32 devices in a mesh: dp: 4 (over x, core), tensor: 4 (over z), proj: 2 (over y).
Axes of the slice: x: 2, y: 2, z: 4, core: 2. Of those that a mesh axis runs over, the one named last changes fastest.
Arguments:
- acts: bfloat16 [40, 1024, 4096], P(('dp', 'proj'), None, 'tensor'), may hold values from -6 to 6
- cotangent: bfloat16 [40, 1024, 4096], P(('dp', 'proj'), None, 'tensor'), may hold values from -6 to 6
- adapter_down: bfloat16 [4096, 128], P('tensor'), may hold values from -0.09375 to 0.09375
- adapter_up: bfloat16 [128, 4096], P(None, 'tensor'), may hold values from -0.09375 to 0.09375
- lengths: int32 [40], P(('dp', 'proj')), may hold values from 256 to 1024, as said below
- projection_rows: int32 [4, 8, 64], P('tensor', ('dp', 'proj')), may hold values from 0 to 127
- projection_blocks: bfloat16 [4, 8, 64, 256, 128], P('tensor', ('dp', 'proj')), may hold values from -2 to 2
Outputs:
- features: float32 [40, 8192], P(('dp', 'proj'), 'tensor')
The draws below stay inside these ranges and needn't reach their ends.
Inputs may be any that keep to these rules, and one draw needn't show every extreme that they name: `lengths`: every sequence has at least 256 tokens; some sequence has exactly 1024.
All inputs are finite; a program needn't handle non-finite values.
Results may differ from the reference program's by a relative error of at most 0.0041.
Values may be sent and summed in bfloat16 or wider, within the bound.
No kernel may reach another device: no remote copies, remote signals or barrier semaphores. Data moves between devices by JAX's collectives and lax.ppermute only.
A program may use at most 128 MiB of HBM per device.

```python
import jax
import jax.numpy as jnp
from jax import lax

MODEL_WIDTH = 4096
ADAPTER_RANK = 128
OB = 128
LEN = 1024
SEQS = 40
NB_OUT = 64
WPARTS = 4
RPARTS = 8
ROWS = 128


def draw_lengths(key, part):
    base = jax.random.randint(key, (SEQS,), LEN // 4, LEN + 1, dtype=jnp.int32)
    longest = jax.random.randint(jax.random.fold_in(key, 7), (), 0, SEQS, dtype=jnp.int32)
    return jnp.where(jnp.arange(SEQS, dtype=jnp.int32) == longest, jnp.int32(LEN), base)


def set_ends(values, own_key, least, largest):
    shape = values.shape
    index_at = [jax.random.randint(jax.random.fold_in(own_key, axis), (), 0, shape[axis]) for axis in range(len(shape))]
    values = values.at[tuple(index_at)].set(least)
    longest = shape.index(max(shape))
    index_at[longest] = (index_at[longest] + 1) % shape[longest]
    return values.at[tuple(index_at)].set(largest)


def shard_levels(rng, extent, shards, least, largest):
    def one(axis_at, blocks):
        draws = jax.random.uniform(jax.random.fold_in(jax.random.fold_in(rng, 6), axis_at), (blocks,), jnp.float32, least / len(shards), largest / len(shards))
        return jnp.repeat(jnp.exp(draws), extent[axis_at] // blocks).reshape((-1,) + (1,) * (len(extent) - axis_at - 1))

    gain = one(*shards[0])
    for cut in shards[1:]:
        gain = gain * one(*cut)
    return gain


def scatter_about(key, extent, width, most, split=(), held_as=jnp.bfloat16):
    array = width * jax.random.normal(key, extent, jnp.float32)
    if split:
        array = array * shard_levels(key, extent, split, -0.22, 0.18)
    return jnp.clip(array, -most, most).astype(held_as)


def setup_inputs(seed: int = 0) -> dict:
    key_list = jax.random.split(jax.random.key(seed), 8)
    return {
        "acts": scatter_about(key_list[0], (SEQS, LEN, MODEL_WIDTH), 1.0, 6.0, ((0, 8), (2, 4))),
        "cotangent": scatter_about(key_list[1], (SEQS, LEN, MODEL_WIDTH), 1.0, 6.0, ((0, 8), (2, 4))),
        "adapter_down": scatter_about(key_list[2], (MODEL_WIDTH, ADAPTER_RANK), MODEL_WIDTH ** -0.5, 0.09375, ((0, 4),)),
        "adapter_up": scatter_about(key_list[3], (ADAPTER_RANK, MODEL_WIDTH), MODEL_WIDTH ** -0.5, 0.09375, ((1, 4),)),
        "lengths": draw_lengths(jax.random.fold_in(key_list[7], 71), 0),
        "projection_rows": set_ends(jax.random.randint(key_list[5], (WPARTS, RPARTS, NB_OUT), 0, ROWS), jax.random.fold_in(key_list[5], 1), 0, ROWS - 1).astype(jnp.int32),
        "projection_blocks": scatter_about(key_list[6], (WPARTS, RPARTS, NB_OUT, 2 * ADAPTER_RANK, OB), (2 * ADAPTER_RANK * WPARTS * RPARTS // LEN) ** -0.5, 2.0, ((0, 4), (1, 8))),
    }


def reference(acts, cotangent, adapter_down, adapter_up, lengths, projection_rows, projection_blocks):
    positions = jnp.arange(LEN, dtype=jnp.int32)

    def one_sequence(inputs_one):
        sequence_activations, sequence_cotangents, seq_len = inputs_one
        weight = (positions < seq_len).astype(jnp.float32) / seq_len.astype(jnp.float32)
        reduced_hidden = jnp.dot(sequence_activations, adapter_down, preferred_element_type=jnp.float32)
        reduced_upstream = jnp.dot(sequence_cotangents, adapter_up.T, preferred_element_type=jnp.float32)
        hidden_w = (reduced_hidden * weight[:, None]).astype(jnp.bfloat16)
        upper_w = (reduced_upstream * weight[:, None]).astype(jnp.bfloat16)
        grad_a = jnp.dot(sequence_activations.T, upper_w, preferred_element_type=jnp.float32)
        grad_b = jnp.dot(sequence_cotangents.T, hidden_w, preferred_element_type=jnp.float32)
        return jnp.concatenate([grad_a, grad_b], axis=1).astype(jnp.bfloat16)

    gradient_list = lax.map(one_sequence, (acts, cotangent, lengths))
    strata = WPARTS * RPARTS
    by_range = gradient_list.reshape(SEQS, strata, ROWS, 2 * ADAPTER_RANK).transpose(1, 0, 2, 3)
    row_pick = projection_rows.reshape(strata, NB_OUT)
    block_list = projection_blocks.reshape(strata, NB_OUT, 2 * ADAPTER_RANK, OB)

    def add_range(running, item_one):
        section, picks, block_one = item_one
        chosen = jnp.take(section, picks, axis=1)
        contrib = jnp.einsum("eok,okc->eoc", chosen.astype(jnp.float32), block_one.astype(jnp.float32),
                             precision=lax.Precision.HIGHEST)
        return running + contrib.reshape(SEQS, NB_OUT * OB), None

    start_sum = jnp.zeros((SEQS, NB_OUT * OB), jnp.float32)
    features, _ = lax.scan(add_range, start_sum, (by_range, row_pick, block_list))
    return features
```

```python
import functools
import jax
import jax.numpy as jnp
from jax import lax
from jax.experimental import pallas as pl
from jax.experimental.pallas import tpu as pltpu
from jax.sharding import PartitionSpec as P


F32, BF16 = jnp.float32, jnp.bfloat16


def after(value, *earlier):
    return lax.optimization_barrier((value,) + earlier)[0]


def low_kernel(acts_ref, cot_ref, down_ref, up_ref, full_ref, half_ref):
    hidden = jnp.dot(acts_ref[...], down_ref[...], preferred_element_type=F32)
    upstream = lax.dot_general(
        cot_ref[...], up_ref[...], (((1,), (1,)), ((), ())), preferred_element_type=F32
    )
    full_ref[0, 0] = hidden
    full_ref[0, 1] = upstream
    half_ref[0, 0] = hidden.astype(BF16)
    half_ref[0, 1] = upstream.astype(BF16)


def low_call(acts, cot, down, up, first, count, chunk, step):
    width, rank = down.shape
    per = chunk // step
    rows = pl.BlockSpec((step, width), lambda i: (first * per + i, 0))
    whole = pl.BlockSpec(memory_space=pltpu.VMEM)
    out = pl.BlockSpec((1, 2, step, rank), lambda i: (i // per, 0, i % per, 0))
    shape = (count, 2, chunk, rank)
    return pl.pallas_call(
        low_kernel,
        grid=(count * per,),
        in_specs=[rows, rows, whole, whole],
        out_specs=[out, out],
        out_shape=[jax.ShapeDtypeStruct(shape, F32), jax.ShapeDtypeStruct(shape, BF16)],
        cost_estimate=pl.CostEstimate(
            flops=4 * count * chunk * width * rank,
            bytes_accessed=4 * count * chunk * width + 12 * count * chunk * rank,
            transcendentals=0,
        ),
        name="low",
    )(acts, cot, down, up)


def grad_kernel(ranges, me_ref, acts_ref, cot_ref, first_ref, second_ref, pick_ref, _, out_ref):
    rank = first_ref.shape[2]
    rows = pick_ref.shape[2]
    block = pl.program_id(0)
    upper = jnp.concatenate([first_ref[1], second_ref[1]], axis=0)
    hidden = jnp.concatenate([first_ref[0], second_ref[0]], axis=0)
    by_token = (((0,), (0,)), ((), ()))
    by_row = (((1,), (1,)), ((), ()))
    grad_a = lax.dot_general(upper, acts_ref[0], by_token, preferred_element_type=F32).astype(BF16)
    grad_b = lax.dot_general(hidden, cot_ref[0], by_token, preferred_element_type=F32).astype(BF16)
    for r in range(ranges):
        slot = jnp.bitwise_xor(block * ranges + r, me_ref[0])
        pick = pick_ref[slot]
        cols = slice(r * rows, (r + 1) * rows)
        out_ref[slot, 0, :, :rank] = lax.dot_general(
            pick, grad_a[:, cols], by_row, preferred_element_type=F32
        ).astype(BF16)
        out_ref[slot, 0, :, rank:] = lax.dot_general(
            pick, grad_b[:, cols], by_row, preferred_element_type=F32
        ).astype(BF16)


def grad_call(me, acts, cot, first, second, pick, buffer, seq, place, cols):
    _, length, width = acts.shape
    parts, picks, rows = pick.shape
    rank = first.shape[2]
    block = pl.BlockSpec((1, length, cols), lambda i, m: (seq, 0, i))
    whole = pl.BlockSpec(memory_space=pltpu.VMEM)
    return pl.pallas_call(
        functools.partial(grad_kernel, cols // rows),
        grid_spec=pltpu.PrefetchScalarGridSpec(
            num_scalar_prefetch=1,
            grid=(width // cols,),
            in_specs=[block, block, whole, whole, whole, pl.BlockSpec(memory_space=pl.ANY)],
            out_specs=pl.BlockSpec((parts, 1, picks, 2 * rank), lambda i, m: (0, place, 0, 0)),
        ),
        out_shape=jax.ShapeDtypeStruct(buffer.shape, BF16),
        input_output_aliases={6: 0},
        cost_estimate=pl.CostEstimate(
            flops=4 * length * width * rank,
            bytes_accessed=4 * length * width + 4 * parts * picks * rank,
            transcendentals=0,
        ),
        name="grad",
    )(me, acts, cot, first, second, pick, buffer)


def project_kernel(count, chosen_ref, block_ref, out_ref):
    for o in range(count):
        out_ref[o] = jnp.dot(chosen_ref[o], block_ref[o], preferred_element_type=F32)


def project_call(chosen, blocks, count):
    outs, rows, depth = chosen.shape
    width = blocks.shape[2]
    return pl.pallas_call(
        functools.partial(project_kernel, count),
        grid=(outs // count,),
        in_specs=[
            pl.BlockSpec((count, rows, depth), lambda i: (i, 0, 0)),
            pl.BlockSpec((count, depth, width), lambda i: (i, 0, 0)),
        ],
        out_specs=pl.BlockSpec((count, rows, width), lambda i: (i, 0, 0)),
        out_shape=jax.ShapeDtypeStruct((outs, rows, width), F32),
        cost_estimate=pl.CostEstimate(
            flops=2 * outs * rows * depth * width,
            bytes_accessed=2 * outs * depth * (rows + width) + 4 * outs * rows * width,
            transcendentals=0,
        ),
        name="project",
    )(chosen, blocks)


GROUP = ("dp", "proj")


def swap(value, bit, size):
    return lax.ppermute(value, GROUP, [(i, i ^ (1 << bit)) for i in range(size)])


def halves(value, bit, bits):
    shape = value.shape
    split = value.reshape((1 << (bits - 1 - bit), 2, 1 << bit) + shape[1:])
    rest = (shape[0] // 2,) + shape[1:]
    return split[:, 0].reshape(rest), split[:, 1].reshape(rest)


def local(acts, cotangent, adapter_down, adapter_up, lengths, projection_rows, projection_blocks):
    seqs, length, width = acts.shape
    rank = adapter_down.shape[1]
    tensor = lax.axis_size("tensor")
    dp, proj = lax.axis_size("dp"), lax.axis_size("proj")
    parts = dp * proj
    bits = parts.bit_length() - 1
    low_bit = proj.bit_length() - 1
    order = list(range(low_bit)) + list(reversed(range(low_bit, bits)))
    me = lax.axis_index(GROUP)
    me1 = me.astype(jnp.int32).reshape(1)
    z = lax.axis_index("tensor")
    edge = (z == 0) | (z == tensor - 1)
    range_rows = width // parts
    outs, depth, out_block = projection_blocks.shape[2:]
    blocks = projection_blocks.reshape(outs, depth, out_block)
    chunk = length // 2
    count = 2 * seqs
    acts2 = acts.reshape(seqs * length, width)
    cot2 = cotangent.reshape(seqs * length, width)

    groups = [(0, 1), (1, 1), (2, 2), (4, 3), (7, count - 7)]
    full, half = {}, {}

    def low(group):
        first, many = groups[group]
        f, b = low_call(acts2, cot2, adapter_down, adapter_up, first, many, chunk, chunk // 2)
        for i in range(many):
            full[first + i], half[first + i] = f[i], b[i]

    side = [(0, 1), (1, 0), (2, 3), (3, 2)]
    middle = [(1, 2), (2, 1)]
    lag = 3
    came_a, came_b, weighted = {}, {}, {}

    picks = projection_rows.reshape(1, outs)
    for bit in range(bits):
        picks = jnp.concatenate([picks, swap(picks, bit, parts)], axis=0)
    pick = (
        picks[:, :, None] == lax.broadcasted_iota(jnp.int32, (parts, outs, range_rows), 2)
    ).astype(BF16)

    def weigh(total, c):
        own = lengths[c // 2]
        at = lax.broadcasted_iota(jnp.int32, total.shape, 1) + (c % 2) * chunk
        return jnp.where(at < own, total * (1.0 / own.astype(F32)), 0.0).astype(BF16)

    token = [None]

    def hold(value):
        return value if token[0] is None else after(value, token[0])

    def start_a(r):
        payload = half[min(r, count - 1)]
        if r >= lag:
            payload = jnp.where(edge, payload, weighted[r - lag])
        came_a[r] = lax.ppermute(payload, "tensor", side)

    def middle_sum(c):
        value = (full[c] + hold(came_a[c]).astype(F32)).astype(BF16)
        token[0] = value
        came_b[c] = lax.ppermute(value, "tensor", middle)

    def total_sum(c):
        total = full[c] + came_a[c].astype(F32) + hold(came_b[c]).astype(F32)
        weighted[c] = weigh(total, c)
        token[0] = weighted[c]

    def hold_weighted(c):
        return jnp.where(edge, came_a[c + lag], weighted[c])

    batches = [(0, 1), (2, 3), tuple(range(4, seqs))]
    batch_of = {s: b for b, members in enumerate(batches) for s in members}
    buffers = [jnp.zeros((parts, len(m), outs, 2 * rank), BF16) for m in batches]

    def grad(seq):
        b = batch_of[seq]
        buffers[b] = grad_call(
            me1, acts, cotangent, hold_weighted(2 * seq), hold_weighted(2 * seq + 1), pick,
            buffers[b], seq, seq - batches[b][0], min(width, 512),
        )

    def exchange(b):
        value = buffers[b]
        value = value.reshape((parts, 1) + value.shape[1:])
        for bit in order:
            left = value.shape[0].bit_length() - 1
            place = sum(1 for other in todo(bit) if other < bit)
            keep, send = halves(value, place, left)
            value = jnp.concatenate([keep, swap(send, bit, parts)], axis=1)
        return value[0]

    def todo(bit):
        return order[order.index(bit):]

    def contribution(value):
        sources, many = value.shape[:2]
        rows = value.reshape(sources * many, outs, depth).transpose(1, 0, 2)
        out = project_call(rows, blocks, min(outs, 8))
        return out.transpose(1, 0, 2).reshape(sources, many, outs, out_block)

    def reduce_group(value):
        for step in reversed(range(bits)):
            bit = order[step]
            keep, send = value[: value.shape[0] // 2], value[value.shape[0] // 2:]
            value = keep + swap(send, bit, parts)
        return value[0]

    def reduce_tensor(value):
        many = value.shape[0]
        value = value.reshape(many, tensor, outs // tensor, out_block)
        own = lax.dynamic_index_in_dim(value, z, 1, False)
        for k in range(1, tensor):
            send = lax.dynamic_index_in_dim(value, jnp.bitwise_xor(z, k), 1, False)
            own = own + lax.ppermute(send, "tensor", [(i, i ^ k) for i in range(tensor)])
        return own.reshape(many, outs // tensor * out_block)

    low(0)
    start_a(0)
    low(1)
    start_a(1)
    low(2)
    results = {}
    for r in range(1, count + lag + 1):
        if r - 1 < count:
            middle_sum(r - 1)
        if 0 <= r - 2 < count:
            total_sum(r - 2)
        if r == 1:
            low(3)
        if r == 2:
            low(4)
        if r + 1 < count + lag:
            start_a(r + 1)
        done = r - 1 - lag
        if done >= 1 and done % 2 == 1:
            seq = done // 2
            grad(seq)
            b = batch_of[seq]
            if seq == batches[b][-1]:
                results[b] = reduce_group(contribution(exchange(b)))
    value = jnp.concatenate([results[b] for b in range(len(batches))], axis=0)
    return reduce_tensor(value)


def solution(mesh):
    placed = (
        P(("dp", "proj"), None, "tensor"),
        P(("dp", "proj"), None, "tensor"),
        P("tensor", None),
        P(None, "tensor"),
        P(("dp", "proj")),
        P("tensor", ("dp", "proj"), None),
        P("tensor", ("dp", "proj"), None, None, None),
    )
    return jax.shard_map(
        local, mesh=mesh, in_specs=placed, out_specs=P(("dp", "proj"), "tensor"), check_vma=False
    )
```

```python
import functools
import jax
import jax.numpy as jnp
from jax import lax
from jax.experimental import pallas as pl
from jax.experimental.pallas import tpu as pltpu
from jax.sharding import PartitionSpec as P


F32, BF16 = jnp.float32, jnp.bfloat16


def after(value, *earlier):
    return lax.optimization_barrier((value,) + earlier)[0]


def far_of(value):
    return pltpu.with_memory_space_constraint(value, pltpu.HBM)


def low_kernel(plan, acts_ref, cot_ref, down_ref, up_ref, *rest):
    seq, start, chunks, chunk, pieces, first = plan
    out = rest[: 2 * chunks]
    acts_buf, cot_buf, down_buf, up_buf, sems = rest[2 * chunks:]
    size = chunk // pieces
    copies = []
    if first:
        copies.append(pltpu.make_async_copy(down_ref, down_buf, sems.at[0]))
        copies.append(pltpu.make_async_copy(up_ref, up_buf, sems.at[1]))
        down_ref, up_ref = down_buf, up_buf
    for i in range(chunks * pieces):
        rows = pl.ds(start + i * size, size)
        at = pl.ds(i * size, size)
        for ref, buf, sem in ((acts_ref, acts_buf, 2 + 2 * i), (cot_ref, cot_buf, 3 + 2 * i)):
            copies.append(
                pltpu.make_async_copy(ref.at[seq, rows, :], buf.at[at, :], sems.at[sem])
            )
    for copy in copies:
        copy.start()
    copies = iter(copies)
    if first:
        next(copies).wait()
        next(copies).wait()
    for i in range(chunks):
        full_ref, half_ref = out[2 * i: 2 * i + 2]
        for p in range(pieces):
            at = slice(p * size, (p + 1) * size)
            rows = slice((i * pieces + p) * size, (i * pieces + p + 1) * size)
            next(copies).wait()
            value = jnp.dot(acts_buf[rows, :], down_ref[...], preferred_element_type=F32)
            full_ref[0, at, :] = value
            half_ref[0, at, :] = value.astype(BF16)
            next(copies).wait()
            value = lax.dot_general(
                cot_buf[rows, :], up_ref[...], (((1,), (1,)), ((), ())), preferred_element_type=F32
            )
            full_ref[1, at, :] = value
            half_ref[1, at, :] = value.astype(BF16)


def low_call(acts, cot, down, up, seq, start, chunks, chunk, pieces, first):
    width, rank = down.shape
    whole = pl.BlockSpec(memory_space=pltpu.VMEM)
    far = pl.BlockSpec(memory_space=pltpu.HBM)
    shapes = [
        jax.ShapeDtypeStruct((2, chunk, rank), F32), jax.ShapeDtypeStruct((2, chunk, rank), BF16)
    ] * chunks
    small = far if first else whole
    return pl.pallas_call(
        functools.partial(low_kernel, (seq, start, chunks, chunk, pieces, first)),
        in_specs=[far, far, small, small],
        out_specs=[whole] * len(shapes),
        out_shape=shapes,
        scratch_shapes=[
            pltpu.VMEM((chunks * chunk, width), BF16),
            pltpu.VMEM((chunks * chunk, width), BF16),
            pltpu.VMEM(down.shape, BF16),
            pltpu.VMEM(up.shape, BF16),
            pltpu.SemaphoreType.DMA((2 + 2 * chunks * pieces,)),
        ],
        compiler_params=pltpu.CompilerParams(vmem_limit_bytes=16 << 20),
        cost_estimate=pl.CostEstimate(
            flops=4 * chunks * chunk * width * rank,
            bytes_accessed=4 * chunks * chunk * width + 12 * chunks * chunk * rank,
            transcendentals=0,
        ),
        name="low",
    )(far_of(acts), far_of(cot), *((far_of(down), far_of(up)) if first else (down, up)))


def grad_kernel(seq, cols, slots_ref, acts_ref, cot_ref, low0, low1, pick_ref, *rest):
    out_ref, acts_buf, cot_buf, sems = rest[-4:]
    rank = low0.shape[2]
    length, width = acts_buf.shape
    rows = pick_ref.shape[2]
    half = length // 2
    by_token = (((0,), (0,)), ((), ()))
    by_row = (((1,), (1,)), ((), ()))
    copies = []
    for i in range(width // cols):
        at = pl.ds(i * cols, cols)
        for ref, buf, sem in ((acts_ref, acts_buf, 2 * i), (cot_ref, cot_buf, 2 * i + 1)):
            copies.append(pltpu.make_async_copy(ref.at[seq, :, at], buf.at[:, at], sems.at[sem]))
    for copy in copies:
        copy.start()

    def product(which, buf, at):
        return (
            lax.dot_general(low0[which], buf[:half, at], by_token, preferred_element_type=F32)
            + lax.dot_general(low1[which], buf[half:, at], by_token, preferred_element_type=F32)
        ).astype(BF16)

    for i in range(width // cols):
        at = slice(i * cols, (i + 1) * cols)
        copies[2 * i].wait()
        grad_a = product(1, acts_buf, at)
        copies[2 * i + 1].wait()
        grad_b = product(0, cot_buf, at)
        for r in range(cols // rows):
            slot = slots_ref[i * (cols // rows) + r]
            pick = pick_ref[slot]
            inner = slice(r * rows, (r + 1) * rows)
            out_ref[slot, 0, :, :rank] = lax.dot_general(
                pick, grad_a[:, inner], by_row, preferred_element_type=F32
            ).astype(BF16)
            out_ref[slot, 0, :, rank:] = lax.dot_general(
                pick, grad_b[:, inner], by_row, preferred_element_type=F32
            ).astype(BF16)


def grad_call(slots, acts, cot, first, second, pick, buffer, seq, place, many, cols):
    _, length, width = acts.shape
    parts, picks, rows = pick.shape
    rank = first.shape[2]
    whole = pl.BlockSpec(memory_space=pltpu.VMEM)
    far = pl.BlockSpec(memory_space=pltpu.HBM)
    chained = buffer is not None
    extra = [pl.BlockSpec(memory_space=pl.ANY)] if chained else []
    return pl.pallas_call(
        functools.partial(grad_kernel, seq, cols),
        grid_spec=pltpu.PrefetchScalarGridSpec(
            num_scalar_prefetch=1,
            grid=(1,),
            in_specs=[far, far, whole, whole, whole] + extra,
            out_specs=pl.BlockSpec((parts, 1, picks, 2 * rank), lambda i, m: (0, place, 0, 0)),
            scratch_shapes=[
                pltpu.VMEM((length, width), BF16),
                pltpu.VMEM((length, width), BF16),
                pltpu.SemaphoreType.DMA((2 * (width // cols),)),
            ],
        ),
        out_shape=jax.ShapeDtypeStruct((parts, many, picks, 2 * rank), BF16),
        input_output_aliases={6: 0} if chained else {},
        compiler_params=pltpu.CompilerParams(vmem_limit_bytes=20 << 20),
        cost_estimate=pl.CostEstimate(
            flops=4 * length * width * rank,
            bytes_accessed=4 * length * width + 4 * parts * picks * rank,
            transcendentals=0,
        ),
        name="grad",
    )(slots, far_of(acts), far_of(cot), first, second, pick, *([buffer] if chained else []))


def project_kernel(count, chosen_ref, block_ref, out_ref):
    for o in range(count):
        out_ref[:, o, :] = jnp.dot(chosen_ref[:, o, :], block_ref[o], preferred_element_type=F32)


def project_call(chosen, blocks, count):
    rows, outs, depth = chosen.shape
    width = blocks.shape[2]
    return pl.pallas_call(
        functools.partial(project_kernel, count),
        grid=(outs // count,),
        in_specs=[
            pl.BlockSpec((rows, count, depth), lambda i: (0, i, 0)),
            pl.BlockSpec((count, depth, width), lambda i: (i, 0, 0)),
        ],
        out_specs=pl.BlockSpec((rows, count, width), lambda i: (0, i, 0)),
        out_shape=jax.ShapeDtypeStruct((rows, outs, width), F32),
        compiler_params=pltpu.CompilerParams(vmem_limit_bytes=24 << 20),
        cost_estimate=pl.CostEstimate(
            flops=2 * outs * rows * depth * width,
            bytes_accessed=2 * outs * depth * (rows + width) + 4 * outs * rows * width,
            transcendentals=0,
        ),
        name="project",
    )(chosen, blocks)


GROUP = ("dp", "proj")


def swap(value, bit, size):
    return lax.ppermute(value, GROUP, [(i, i ^ (1 << bit)) for i in range(size)])


def local(acts, cotangent, adapter_down, adapter_up, lengths, projection_rows, projection_blocks):
    seqs, length, width = acts.shape
    rank = adapter_down.shape[1]
    tensor = lax.axis_size("tensor")
    dp, proj = lax.axis_size("dp"), lax.axis_size("proj")
    parts = dp * proj
    bits = parts.bit_length() - 1
    low_bit = proj.bit_length() - 1
    order = list(range(low_bit)) + list(reversed(range(low_bit, bits)))
    me = lax.axis_index(GROUP).astype(jnp.int32)
    z = lax.axis_index("tensor")
    edge = (z == 0) | (z == tensor - 1)
    range_rows = width // parts
    outs, depth, out_block = projection_blocks.shape[2:]
    blocks = projection_blocks.reshape(outs, depth, out_block)
    chunk = length // 2
    count = 2 * seqs
    apart = jnp.bitwise_xor(jnp.arange(parts, dtype=jnp.int32), me)
    slots = sum(((apart >> bit) & 1) << (bits - 1 - i) for i, bit in enumerate(order))

    token = [None]

    def hold(value):
        return value if token[0] is None else after(value, token[0])

    def mark(value):
        token[0] = value
        return value

    full, half = {}, {}

    def low(first, many):
        opening = first == 0
        with jax.named_scope(f"low{first}"):
            out = low_call(
                acts, cotangent, hold(adapter_down), adapter_up, first // 2,
                (first % 2) * chunk, many, chunk, 2, opening,
            )
        for i in range(many):
            full[first + i], half[first + i] = out[2 * i: 2 * i + 2]
        mark(half[first])

    side = [(0, 1), (1, 0), (2, 3), (3, 2)]
    middle = [(1, 2), (2, 1)]
    lag = 3
    came_a, came_b, payload = {}, {}, {}

    own_length = jnp.broadcast_to(lengths[:, None, None], (seqs, 1, rank))
    own_scale = 1.0 / own_length.astype(F32)
    own_length, own_scale = lax.optimization_barrier((own_length, own_scale))

    def start_a(r):
        value = half[min(r, count - 1)]
        if r >= lag:
            c = r - lag
            total = full[c] + came_a[c].astype(F32) + hold(came_b[c]).astype(F32)
            at = lax.broadcasted_iota(jnp.int32, total.shape, 1) + (c % 2) * chunk
            ready = jnp.where(at < own_length[c // 2], total * own_scale[c // 2], 0.0).astype(BF16)
            value = mark(jnp.where(edge, value, ready))
        payload[r] = value
        with jax.named_scope(f"A{r}"):
            came_a[r] = lax.ppermute(value, "tensor", side)

    def start_b(c):
        value = mark((full[c] + hold(came_a[c]).astype(F32)).astype(BF16))
        with jax.named_scope(f"B{c}"):
            came_b[c] = lax.ppermute(value, "tensor", middle)

    def weighted(c):
        return jnp.where(edge, hold(came_a[c + lag]), payload[c + lag])

    pick = []

    def gather_picks():
        picks = projection_rows.reshape(1, outs)
        for bit in reversed(order):
            with jax.named_scope(f"pick{bit}"):
                came = swap(picks, bit, parts)
            yield
            picks = mark(jnp.concatenate([picks, hold(came)], axis=0))
        at = lax.broadcasted_iota(jnp.int32, (parts, outs, range_rows), 2)
        pick.append((picks[:, :, None] == at).astype(BF16))

    batches = [m for m in ((0, 1), (2, 3), tuple(range(4, seqs))) if m]
    batch_of = {s: b for b, members in enumerate(batches) for s in members}
    buffers = [None for _ in batches]

    def grad(seq):
        b = batch_of[seq]
        buffers[b] = mark(grad_call(
            slots, acts, cotangent, weighted(2 * seq), weighted(2 * seq + 1), pick[0],
            buffers[b], seq, seq - batches[b][0], len(batches[b]), min(width, 512),
        ))

    arrived, reduced = {}, {}

    def exchange(b):
        value = buffers[b]
        value = value.reshape((parts, 1) + value.shape[1:])
        for bit in order:
            cut = value.shape[0] // 2
            with jax.named_scope(f"ex{b}_{bit}"):
                came = swap(value[cut:], bit, parts)
            yield
            value = mark(jnp.concatenate([value[:cut], hold(came)], axis=1))
        arrived[b] = value[0]

    def reduce_group(members):
        value = jnp.concatenate([arrived[b] for b in members], axis=1)
        sources, many = value.shape[:2]
        rows = value.reshape(sources * many, outs, depth)
        value = mark(project_call(hold(rows), blocks, min(outs, 32)))
        value = value.reshape(sources, many, outs, out_block)
        for bit in reversed(order):
            cut = value.shape[0] // 2
            with jax.named_scope(f"red{members[0]}_{bit}"):
                came = swap(value[cut:], bit, parts)
            yield
            value = mark(value[:cut] + hold(came))
        reduced[members] = value[0]

    def reduce_tensor(value):
        many = value.shape[0]
        value = value.reshape(many, tensor, outs // tensor, out_block)
        own = lax.dynamic_index_in_dim(value, z, 1, False)
        for k in range(1, tensor):
            send = lax.dynamic_index_in_dim(value, jnp.bitwise_xor(z, k), 1, False)
            own = own + lax.ppermute(send, "tensor", [(i, i ^ k) for i in range(tensor)])
        return own.reshape(many, outs // tensor * out_block)

    def run(task):
        return next(task, None)

    low(0, 1)
    start_a(0)
    low(1, 1)
    start_a(1)
    low(2, 2)
    start_a(2)
    picks_task = gather_picks()
    tasks, started, fresh = [], [], []
    for r in range(1, count + lag + 1):
        if r - 1 < count:
            start_b(r - 1)
        if lag <= r + 1 < count + lag:
            start_a(r + 1)
        if 2 * r + 2 < count:
            low(2 * r + 2, 2)
        if r == 2:
            for _ in picks_task:
                pass
        done = r - 1 - lag
        if done >= 1 and done % 2 == 1:
            seq = done // 2
            grad(seq)
            b = batch_of[seq]
            if seq == batches[b][-1]:
                task = exchange(b)
                run(task)
                fresh.append(task)
        for task in tasks:
            run(task)
        tasks, fresh = tasks + fresh, []
        if 0 in arrived and not started:
            started.append(True)
            task = reduce_group((0,))
            run(task)
            tasks.append(task)
    for _ in range(bits):
        for task in tasks:
            run(task)
    last = tuple(range(1, len(batches)))
    if last:
        for _ in reduce_group(last):
            pass
    value = jnp.concatenate([reduced[m] for m in sorted(reduced)], axis=0)
    return reduce_tensor(value)


def solution(mesh):
    placed = (
        P(("dp", "proj"), None, "tensor"),
        P(("dp", "proj"), None, "tensor"),
        P("tensor", None),
        P(None, "tensor"),
        P(("dp", "proj")),
        P("tensor", ("dp", "proj"), None),
        P("tensor", ("dp", "proj"), None, None, None),
    )
    return jax.shard_map(
        local, mesh=mesh, in_specs=placed, out_specs=P(("dp", "proj"), "tensor"), check_vma=False
    )
```
